32 devices in a mesh: slab: 8 (over z, y), sub: 4 (over x, core).
Axes of the slice: x: 2, y: 2, z: 4, core: 2. Of those that a mesh axis runs over, the one named last changes fastest.
Arguments:
- start: float32 [64, 6, 2, 16, 128], P(('slab', 'sub')), may hold values from -20 to 20
- inv_factor: bfloat16 [1024, 2, 128, 128], P(('slab', 'sub')), as said below
- partner: int32 [64, 6], P(('slab', 'sub')), may hold values from -1 to 63, as said below
- partner_face: int32 [64, 6], P(('slab', 'sub')), may hold values from -1 to 5, as said below
- elem_class: int32 [64, 16], P(('slab', 'sub')), may hold values from 0 to 3
- elem_face: int32 [64, 16], P(('slab', 'sub')), may hold values from 0 to 5
- load_map: bfloat16 [4, 2, 128, 128], replicated, may hold values from -0.375 to 0.375
- trace_map: bfloat16 [4, 2, 128, 128], replicated, may hold values from -0.25 to 0.25
Outputs:
- last_block: float32 [64, 6, 2, 16, 128], P(('slab', 'sub'))
- hessenberg: float32 [4, 5, 16, 16], replicated
The draws below stay inside these ranges and needn't reach their ends.
Inputs may be any that keep to these rules, and one draw needn't show every extreme that they name: Global subdomain s lies on device s // 2 of the joined axes. Across faces 0 and 1 the partner lies on the same device; across face 2 on the device one lower along sub, face 3 one higher along sub, face 4 one lower along slab, face 5 one higher along slab, and -1 exactly where no such device exists. `partner_face`: faces 0 and 1 meet face 0 or 1 of their partner; faces 2, 3, 4, 5 meet faces 3, 2, 5, 4; -1 exactly where partner is -1. `inv_factor`: each factor is lower triangular with a real diagonal of 0.5 to 2 and a small imaginary diagonal.
All inputs are finite; a program needn't handle non-finite values.
Results may differ from the reference program's by a relative error of at most 0.013.
Values sent between devices are 32-bit elements; how exact they have to be, the bound alone decides.
No kernel may reach another device: no remote copies, remote signals or barrier semaphores. Data moves between devices by JAX's collectives and lax.ppermute only.
A program may use at most 64 MiB of HBM per device.

```python
import math
import jax
import jax.numpy as jnp
from jax import lax

SUBDEV = 2
EL = 16
PW = 128
Q = 128
NR = 16
NC = 4
ITERS = 4
NSLAB = 8
NSUB = 4
SUBS_ALL = 64
ELEMS = 1024


def partner_layout():
    global_index = jnp.arange(SUBS_ALL, dtype=jnp.int32)
    device = global_index // SUBDEV
    slab_index = device // NSUB
    sub_index = device % NSUB
    always_there = jnp.ones((SUBS_ALL,), dtype=bool)
    has_partner = jnp.stack([always_there, always_there, sub_index > 0, sub_index < NSUB - 1, slab_index > 0, slab_index < NSLAB - 1], axis=1)
    target_device = device[:, None] + jnp.array([0, 0, -1, 1, -NSUB, NSUB], jnp.int32)[None, :]
    return (has_partner, target_device)


def draw_start(key, part):
    value_key = jax.random.fold_in(key, 53)
    common_key = jax.random.fold_in(key, 59)
    weight_key = jax.random.fold_in(key, 61)
    sign_key = jax.random.fold_in(key, 67)
    full_shape = (SUBS_ALL, 6, 2, NR, Q)
    common_shape = (SUBS_ALL, 6, 2, 1, Q)
    position = jnp.arange(SUBS_ALL, dtype=jnp.float32) / (SUBS_ALL - 1)
    mixing = jax.random.uniform(weight_key, (NR,), jnp.float32, 0.5, 0.95)
    mixing = mixing * jnp.where(jax.random.bernoulli(sign_key, 0.5, (NR,)), 1.0, -1.0)
    values = 0.7 * jnp.clip(jax.random.normal(value_key, full_shape, jnp.float32), -4.0, 4.0)
    common = 0.7 * jnp.clip(jax.random.normal(common_key, common_shape, jnp.float32), -4.0, 4.0)
    growth = jnp.exp(position * math.log(3.0))
    mixed = values + common * mixing[None, None, None, :, None]
    return mixed * growth[:, None, None, None, None]


def draw_partner(key, part):
    has_partner, target_device = partner_layout()
    local_index = jax.random.randint(jax.random.fold_in(key, 17), (SUBS_ALL, 6), 0, SUBDEV, dtype=jnp.int32)
    local_index = local_index.at[SUBS_ALL - 1, 0].set(SUBDEV - 1)
    return jnp.where(has_partner, target_device * SUBDEV + local_index, -1).astype(jnp.int32)


def draw_partner_face(key, part):
    has_partner, target_device = partner_layout()
    inner_face = jax.random.randint(jax.random.fold_in(key, 29), (SUBS_ALL, 6), 0, 2, dtype=jnp.int32)
    opposite = jnp.array([0, 0, 3, 2, 5, 4], jnp.int32)[None, :]
    column = jnp.arange(6, dtype=jnp.int32)[None, :]
    chosen_face = jnp.where(column < 2, inner_face, opposite)
    return jnp.where(has_partner, chosen_face, -1).astype(jnp.int32)


def draw_inv_factor(key, part):
    off_key = jax.random.fold_in(key, 41)
    diag_key = jax.random.fold_in(key, 43)
    imag_key = jax.random.fold_in(key, 47)
    full_shape = (ELEMS, 2, PW, PW)
    spread = jax.random.normal(off_key, full_shape, jnp.float32)
    strict = jnp.tril(jnp.ones((PW, PW), jnp.float32), -1)
    factor = spread * strict * (0.3 / math.sqrt(PW))
    diag_real = jnp.exp(jax.random.uniform(diag_key, (ELEMS, PW), jnp.float32, math.log(0.5), math.log(2.0)))
    diag_imag = 0.2 * jax.random.normal(imag_key, (ELEMS, PW), jnp.float32)
    eye_matrix = jnp.eye(PW, dtype=jnp.float32)
    real_part = factor[:, 0] + diag_real[:, :, None] * eye_matrix
    imag_part = factor[:, 1] + diag_imag[:, :, None] * eye_matrix
    return jnp.stack([real_part, imag_part], axis=1).astype(jnp.bfloat16)


def set_ends(values, key, least, high):
    place = [jax.random.randint(jax.random.fold_in(key, axis), (), 0, length) for axis, length in enumerate(values.shape)]
    widest = values.shape.index(max(values.shape))
    next_to = place[:widest] + [(place[widest] + 1) % values.shape[widest]] + place[widest + 1:]
    return values.at[tuple(place)].set(least).at[tuple(next_to)].set(high)


def gaussian(rng, extent, scale, reach, held_as=jnp.bfloat16):
    values = scale * jax.random.normal(rng, extent, jnp.float32)
    return jnp.clip(values, min=-reach, max=reach).astype(held_as)


def setup_inputs(seed: int = 0) -> dict:
    streams_of = jax.random.split(jax.random.key(seed), 9)
    return {
        "start": draw_start(jax.random.fold_in(streams_of[8], 71), 0),
        "inv_factor": draw_inv_factor(jax.random.fold_in(streams_of[8], 71), 0),
        "partner": draw_partner(jax.random.fold_in(streams_of[8], 71), 0),
        "partner_face": draw_partner_face(jax.random.fold_in(streams_of[8], 71), 0),
        "elem_class": set_ends(jax.random.randint(streams_of[4], (SUBS_ALL, EL), 0, NC), jax.random.fold_in(streams_of[4], 1), 0, NC - 1).astype(jnp.int32),
        "elem_face": set_ends(jax.random.randint(streams_of[5], (SUBS_ALL, EL), 0, 6), jax.random.fold_in(streams_of[5], 1), 0, 5).astype(jnp.int32),
        "load_map": gaussian(streams_of[6], (NC, 2, PW, Q), (2 * Q) ** -0.5, 0.375),
        "trace_map": gaussian(streams_of[7], (NC, 2, Q, PW), (4 * PW) ** -0.5, 0.25),
    }


HIGHEST_PRECISION = lax.Precision.HIGHEST

def load_terms(vector_b, load_map):
    layout = 'cpq,sfrq->sfcrp'
    map_real = load_map[:, 0].astype(jnp.float32)
    map_imag = load_map[:, 1].astype(jnp.float32)
    vec_real = vector_b[:, :, 0].astype(jnp.float32)
    vec_imag = vector_b[:, :, 1].astype(jnp.float32)
    real_part = jnp.einsum(layout, map_real, vec_real, precision=HIGHEST_PRECISION) - jnp.einsum(layout, map_imag, vec_imag, precision=HIGHEST_PRECISION)
    imag_part = jnp.einsum(layout, map_real, vec_imag, precision=HIGHEST_PRECISION) + jnp.einsum(layout, map_imag, vec_real, precision=HIGHEST_PRECISION)
    return jnp.stack([real_part, imag_part], axis=3)

def factor_apply(factor_real, factor_imag, vector_b, adjoint):
    vec_real = vector_b[:, 0].astype(jnp.float32)
    vec_imag = vector_b[:, 1].astype(jnp.float32)
    if adjoint:
        layout = 'eji,erj->eri'
        real_part = jnp.einsum(layout, factor_real, vec_real, precision=HIGHEST_PRECISION) + jnp.einsum(layout, factor_imag, vec_imag, precision=HIGHEST_PRECISION)
        imag_part = jnp.einsum(layout, factor_real, vec_imag, precision=HIGHEST_PRECISION) - jnp.einsum(layout, factor_imag, vec_real, precision=HIGHEST_PRECISION)
    else:
        layout = 'eij,erj->eri'
        real_part = jnp.einsum(layout, factor_real, vec_real, precision=HIGHEST_PRECISION) - jnp.einsum(layout, factor_imag, vec_imag, precision=HIGHEST_PRECISION)
        imag_part = jnp.einsum(layout, factor_real, vec_imag, precision=HIGHEST_PRECISION) + jnp.einsum(layout, factor_imag, vec_real, precision=HIGHEST_PRECISION)
    return jnp.stack([real_part, imag_part], axis=1)

def trace_apply(matrix, coefficients):
    layout = 'qp,serp->serq'
    map_real = matrix[0].astype(jnp.float32)
    map_imag = matrix[1].astype(jnp.float32)
    vec_real = coefficients[:, :, 0].astype(jnp.float32)
    vec_imag = coefficients[:, :, 1].astype(jnp.float32)
    real_part = jnp.einsum(layout, map_real, vec_real, precision=HIGHEST_PRECISION) - jnp.einsum(layout, map_imag, vec_imag, precision=HIGHEST_PRECISION)
    imag_part = jnp.einsum(layout, map_real, vec_imag, precision=HIGHEST_PRECISION) + jnp.einsum(layout, map_imag, vec_real, precision=HIGHEST_PRECISION)
    return jnp.stack([real_part, imag_part], axis=2)

def apply_operator(vector, factor_real, factor_imag, partner, partner_face, elem_class, elem_face, load_map, trace_map):
    sub_count = vector.shape[0]
    vector_b = vector.astype(jnp.bfloat16)
    loads = load_terms(vector_b, load_map).reshape(sub_count, 6 * NC, 2, NR, PW)
    pick_slot = (elem_face * NC + elem_class).astype(jnp.int32)
    chosen = jnp.take_along_axis(loads, pick_slot[:, :, None, None, None], axis=1)
    chosen_b = chosen.astype(jnp.bfloat16).reshape(sub_count * EL, 2, NR, PW)
    middle = factor_apply(factor_real, factor_imag, chosen_b, False).astype(jnp.bfloat16)
    coefficients = factor_apply(factor_real, factor_imag, middle, True).astype(jnp.bfloat16).reshape(sub_count, EL, 2, NR, PW)
    accumulated = jnp.zeros((sub_count, EL, 2, NR, Q), jnp.float32)
    for kind_index in range(NC):
        contribution = trace_apply(trace_map[kind_index], coefficients)
        accumulated = jnp.where((elem_class == kind_index)[:, :, None, None, None], contribution, accumulated)
    face_onehot = (elem_face[:, :, None] == jnp.arange(6, dtype=jnp.int32)[None, None, :]).astype(jnp.float32)
    outgoing = jnp.einsum('sef,sexrq->sfxrq', face_onehot, accumulated, precision=HIGHEST_PRECISION) - vector
    flat_traces = outgoing.reshape(sub_count * 6, 2, NR, Q)
    has_partner = partner >= 0
    source_slot = jnp.where(has_partner, partner * 6 + partner_face, 0).astype(jnp.int32)
    incoming = jnp.where(has_partner[:, :, None, None, None], flat_traces[source_slot], 0.0)
    return vector - incoming

def normalize(vector, gram_matrix):
    low_factor = jnp.linalg.cholesky(gram_matrix)
    identity = jnp.eye(gram_matrix.shape[0], dtype=jnp.float32)
    inverse = lax.linalg.triangular_solve(low_factor, identity, left_side=True, lower=True)
    return (jnp.einsum('sfxaq,ba->sfxbq', vector, inverse, precision=HIGHEST_PRECISION), low_factor.T)

def reference(start, inv_factor, partner, partner_face, elem_class, elem_face, load_map, trace_map):
    entry_count = start.size // NR
    factor_real = inv_factor[:, 0].astype(jnp.float32)
    factor_imag = inv_factor[:, 1].astype(jnp.float32)
    start_gram = jnp.einsum('sfxiq,sfxjq->ij', start, start, precision=HIGHEST_PRECISION) / entry_count
    basis_block, upper_factor = normalize(start, start_gram)
    blocks = [basis_block]
    hessenberg = jnp.zeros((ITERS, ITERS + 1, NR, NR), jnp.float32)
    for number in range(ITERS):
        image_block = apply_operator(blocks[-1], factor_real, factor_imag, partner, partner_face, elem_class, elem_face, load_map, trace_map)
        stacked = jnp.stack(blocks)
        projection = jnp.einsum('ksfxiq,sfxjq->kij', stacked, image_block, precision=HIGHEST_PRECISION) / entry_count
        image_block = image_block - jnp.einsum('ksfxaq,kab->sfxbq', stacked, projection, precision=HIGHEST_PRECISION)
        gram_matrix = jnp.einsum('sfxiq,sfxjq->ij', image_block, image_block, precision=HIGHEST_PRECISION) / entry_count
        basis_block, upper_factor = normalize(image_block, gram_matrix)
        hessenberg = hessenberg.at[number, :number + 1].set(projection)
        hessenberg = hessenberg.at[number, number + 1].set(upper_factor)
        blocks.append(basis_block)
    return (blocks[-1], hessenberg)
```

```python
import functools

import jax
import jax.numpy as jnp
from jax import lax
from jax.experimental import pallas as pl
from jax.experimental.pallas import tpu as pltpu
from jax.sharding import PartitionSpec as P

ITERS = 4
STEP_SCALE = 2.0**-8
KEPT = (0, 1, 3, 5)
GROUP = 4

F32 = jnp.float32
BF16 = jnp.bfloat16
HIGHEST = lax.Precision.HIGHEST


def dot(a, b, transposed=False, precision=None):
    dims = (((1,), (1 if transposed else 0,)), ((), ()))
    return lax.dot_general(a, b, dims, precision=precision, preferred_element_type=F32)


def two_parts(x):
    high = x.astype(BF16)
    return high, (x - high.astype(F32)).astype(BF16)


def doubled(x):
    return jnp.concatenate(two_parts(x), axis=0)


def compose(faces, slot_of, face_ref, class_ref, inv_ref, load_ref, trace_ref, add_to, scratch):
    first_ref, last_ref, held, sems, ids, part = scratch
    subs, elems = face_ref.shape
    half = load_ref.shape[2]

    def chosen(face):
        hit = face == faces[0]
        for f in faces[1:]:
            hit = hit | (face == f)
        return hit

    def fetch(e, count):
        hit = chosen(face_ref[e // elems, e % elems])

        @pl.when(hit)
        def _():
            ids[count] = e
            pltpu.make_async_copy(inv_ref.at[e], held.at[count], sems.at[count]).start()

        return count + hit.astype(jnp.int32)

    total = lax.fori_loop(0, subs * elems, fetch, jnp.int32(0))

    for c in range(load_ref.shape[0]):
        for x in range(2):
            first_ref[c, :, x * half : (x + 1) * half] = load_ref[c, x].astype(F32).T.astype(BF16)
        last_ref[c, :half, :half] = trace_ref[c, 0]
        last_ref[c, :half, half:] = -trace_ref[c, 1]
        last_ref[c, half:, :half] = trace_ref[c, 1]
        last_ref[c, half:, half:] = trace_ref[c, 0]

    def group(g, carry):
        for u in range(GROUP):
            at = g * GROUP + u

            @pl.when(at < total)
            def _():
                pltpu.make_async_copy(inv_ref.at[0], held.at[at], sems.at[at]).wait()

        places = []
        for u in range(GROUP):
            at = jnp.minimum(g * GROUP + u, total - 1)
            e = ids[at]
            face = face_ref[e // elems, e % elems]
            kind = class_ref[e // elems, e % elems]
            real = held[at, 0]
            imag = held[at, 1]
            wide = jnp.concatenate(
                [
                    jnp.concatenate([real, -imag], axis=1),
                    jnp.concatenate([imag, real], axis=1),
                ],
                axis=0,
            )
            out = dot(first_ref[kind], wide, True)
            out = dot(doubled(out), wide)
            out = dot(doubled(out[:half] + out[half:]), last_ref[kind], True)
            part[u] = out[:half] + out[half:]
            places.append((e // elems, face))
        for u in range(GROUP):
            add_to(places[u][0], places[u][1], jnp.where(g * GROUP + u < total, part[u], 0.0))
        return carry

    lax.fori_loop(0, (total + GROUP - 1) // GROUP, group, 0)


def compose_sent(face_ref, class_ref, partner_ref, inv_ref, load_ref, trace_ref, start_ref,
                 sub_ref, slab_ref, sum_ref, *scratch):
    subs = face_ref.shape[0]
    half = load_ref.shape[2]
    rhs = start_ref.shape[3]
    sum_ref[...] = jnp.zeros_like(sum_ref)

    def add_to(s, face, value):
        at = s * 2 + (face == 4).astype(jnp.int32)
        sum_ref[at] = sum_ref[at] + value

    compose((2, 4), None, face_ref, class_ref, inv_ref, load_ref, trace_ref, add_to, scratch)
    for out_ref, face in ((sub_ref, 2), (slab_ref, 4)):
        for s in range(subs):
            out_ref[s, :half] = sum_ref[s * 2 + (face == 4)]
            out_ref[s, half : half + rhs, :half] = start_ref[s, face, 0]
            out_ref[s, half : half + rhs, half:] = start_ref[s, face, 1]
            partner = partner_ref[s, face]
            there = (partner >= 0).astype(F32)
            local = jnp.where(partner >= 0, partner % subs, 0).astype(F32)
            out_ref[s, half + rhs : half + rhs + 8] = jnp.full((8, 2 * half), local, F32)
            out_ref[s, half + rhs + 8 : half + rhs + 16] = jnp.full((8, 2 * half), there, F32)


def spread(rows):
    half = rows.shape[0]
    lower = jnp.concatenate([-rows[:, half:], rows[:, :half]], axis=1)
    return two_parts(jnp.concatenate([rows, lower], axis=0))


def compose_kept(face_ref, class_ref, inv_ref, load_ref, trace_ref, high_ref, low_ref, sum_ref, *scratch):
    sum_ref[...] = jnp.zeros_like(sum_ref)

    def add_to(s, face, value):
        place = jnp.where(face == 3, 2, jnp.where(face == 5, 3, face))
        at = s * len(KEPT) + place
        sum_ref[at] = sum_ref[at] + value

    compose(KEPT, None, face_ref, class_ref, inv_ref, load_ref, trace_ref, add_to, scratch)
    for at in range(sum_ref.shape[0]):
        high, low = spread(sum_ref[at])
        high_ref[at] = high
        low_ref[at] = low


def krylov(partner_ref, partner_face_ref, high_ref, low_ref, from_sub_ref, from_slab_ref, start_ref,
           gram_ref, kept_ref, to_sub_ref, to_slab_ref, remote_high, remote_low, remote, out_ref):
    subs, _, _, rhs, half = start_ref.shape
    kept = len(KEPT)
    own = subs * kept
    sources = (from_sub_ref, from_slab_ref)

    for d in range(2):
        for t in range(subs):
            high, low = spread(sources[d][t, :half])
            remote_high[d * subs + t] = high
            remote_low[d * subs + t] = low
            remote[d * subs + t, :rhs] = sources[d][t, half : half + rhs]
    for s in range(subs):
        for i, face in enumerate(KEPT):
            kept_ref[s * kept + i, :rhs, :half] = start_ref[s, face, 0]
            kept_ref[s * kept + i, :rhs, half:] = start_ref[s, face, 1]

    def leaving(x, high, low):
        top, rest = two_parts(x)
        both = dot(jnp.concatenate([top, rest], axis=0), high)
        return both[:rhs] + both[rhs:] + dot(top, low) - x

    for k in range(ITERS):
        now = slice(k * rhs, (k + 1) * rhs)
        later = slice((k + 1) * rhs, (k + 2) * rhs)
        for at in range(own):
            out_ref[at] = leaving(kept_ref[at, now], high_ref[at], low_ref[at]) * STEP_SCALE
        for at in range(2 * subs):
            out_ref[own + at] = (
                leaving(remote[at, now], remote_high[at], remote_low[at]) * STEP_SCALE
            )
        for s in range(subs):
            for i, face in enumerate(KEPT):
                partner = partner_ref[s, face]
                local = partner % subs
                if i < 2:
                    local = local * 2 + partner_face_ref[s, face]
                    places = [p * kept + f for p in range(subs) for f in range(2)]
                else:
                    places = [own + (i - 2) * subs + p for p in range(subs)]
                value = out_ref[places[0]]
                for p in range(1, len(places)):
                    value = jnp.where(local == p, out_ref[places[p]], value)
                kept_ref[s * kept + i, later] = jnp.where(partner >= 0, value, 0.0)
        for d in range(2):
            for t in range(subs):
                local = sources[d][t, half + rhs : half + rhs + 1]
                there = sources[d][t, half + rhs + 8 : half + rhs + 9]
                value = out_ref[2 + d]
                for s in range(1, subs):
                    value = jnp.where(local > s - 0.5, out_ref[s * kept + 2 + d], value)
                remote[d * subs + t, later] = jnp.where(there > 0.5, value, 0.0)

    total = None
    for at in range(own + 2 * subs):
        rows = kept_ref[at] if at < own else remote[at - own]
        term = dot(rows, rows, True, HIGHEST)
        total = term if total is None else total + term
    first = total[:rhs, :rhs]
    for face in (2, 4):
        for s in range(subs):
            alone = jnp.where(partner_ref[s, face] < 0, 1.0, 0.0)
            for x in range(2):
                rows = start_ref[s, face, x] * alone
                first = first + dot(rows, rows, True, HIGHEST)
    for d, to_ref in enumerate((to_sub_ref, to_slab_ref)):
        for t in range(subs):
            to_ref[t] = remote[d * subs + t, rhs:]

    gram_ref[...] = jnp.zeros_like(gram_ref)
    for row, (blocks) in enumerate(((4, 1, 0), (3, 2))):
        lane = 0
        for i in blocks:
            width = (i + 1) * rhs
            piece = first if i == 0 else total[i * rhs : (i + 1) * rhs, :width]
            gram_ref[row * rhs : (row + 1) * rhs, lane : lane + width] = piece
            lane += width


def finish(count, gram_ref, kept_ref, back_sub_ref, back_slab_ref, start_ref, last_ref, hess_ref,
           upper_ref, inverse_ref):
    subs, _, _, rhs, half = start_ref.shape
    kept = len(KEPT)
    size = (ITERS + 1) * rhs
    lanes = 128
    offset = {}
    for row, (blocks) in enumerate(((4, 1, 0), (3, 2))):
        lane = 0
        for i in blocks:
            offset[i] = (row, lane)
            lane += (i + 1) * rhs
    upper_ref[...] = jnp.zeros_like(upper_ref)
    for i in range(ITERS + 1):
        row, lane = offset[i]
        width = (i + 1) * rhs
        upper_ref[i * rhs : (i + 1) * rhs, :width] = (
            gram_ref[row * rhs : (row + 1) * rhs, lane : lane + width] / count
        )
    lower = upper_ref[...]
    down = lax.broadcasted_iota(jnp.int32, (lanes, lanes), 0)
    across = lax.broadcasted_iota(jnp.int32, (lanes, lanes), 1)
    square = jnp.where(down >= across, lower, 0.0)
    full = jnp.where(down >= across, lower, square.T)

    blocks = size // 8
    work = [full[8 * i : 8 * i + 8] for i in range(blocks)]
    side = [
        (down[8 * i : 8 * i + 8] == across[8 * i : 8 * i + 8]).astype(F32) for i in range(blocks)
    ]
    sub_row = lax.broadcasted_iota(jnp.int32, (8, lanes), 0)
    for j in range(size):
        i, r = divmod(j, 8)
        row = jnp.broadcast_to(work[i][r : r + 1], (8, lanes))
        other = jnp.broadcast_to(side[i][r : r + 1], (8, lanes))
        pivot = jnp.broadcast_to(row[:, j : j + 1], (8, lanes))
        root = lax.rsqrt(pivot)
        scaled = row * root
        other = other * root
        upper_ref[j : j + 1, :] = scaled[:1]
        inverse_ref[j : j + 1, :] = other[:1]
        for m in range(i, blocks):
            if 8 * m + 7 <= j:
                continue
            column = jnp.broadcast_to(work[m][:, j : j + 1], (8, lanes)) * root
            if m == i:
                column = jnp.where(sub_row > r, column, 0.0)
            work[m] = work[m] - column * scaled
            side[m] = side[m] - column * other
    upper_ref[size:, :] = jnp.zeros((lanes - size, lanes), F32)
    inverse_ref[size:, :] = jnp.zeros((lanes - size, lanes), F32)

    upper = jnp.where(down <= across, upper_ref[...], 0.0)
    inverse = jnp.where(down >= across, inverse_ref[...], 0.0)
    shifted = jnp.concatenate([upper[:, rhs:], jnp.zeros((lanes, rhs), F32)], axis=1)
    moved = dot(shifted, inverse, True, HIGHEST) * (1.0 / STEP_SCALE)
    unit = (down[:rhs, :rhs] == across[:rhs, :rhs]).astype(F32)
    for k in range(ITERS):
        for j in range(ITERS + 1):
            if j > k + 1:
                hess_ref[k, j] = jnp.zeros((rhs, rhs), F32)
                continue
            block = moved[j * rhs : (j + 1) * rhs, k * rhs : (k + 1) * rhs]
            block = block if (j + k) % 2 else -block
            hess_ref[k, j] = block + unit if j == k else block

    mix = inverse[ITERS * rhs : size, :size]
    for s in range(subs):
        for i, face in enumerate(KEPT):
            value = dot(mix, kept_ref[s * kept + i], False, HIGHEST)
            last_ref[s, face, 0] = value[:, :half]
            last_ref[s, face, 1] = value[:, half:]
        for face, back_ref in ((2, back_sub_ref), (4, back_slab_ref)):
            first = jnp.concatenate([start_ref[s, face, 0], start_ref[s, face, 1]], axis=1)
            rows = jnp.concatenate([first, back_ref[s]], axis=0)
            value = dot(mix, rows, False, HIGHEST)
            last_ref[s, face, 0] = value[:, :half]
            last_ref[s, face, 1] = value[:, half:]


def summed(x, axes):
    for axis in axes:
        count, stride = lax.axis_size(axis), 1
        while stride < count:
            rest = count // stride
            ways = next(p for p in range(2, rest + 1) if rest % p == 0)
            received = []
            for d in range(1, ways):
                pairs = []
                for i in range(count):
                    digit = (i // stride) % ways
                    pairs.append((i, i + ((digit + d) % ways - digit) * stride))
                received.append(lax.ppermute(x, axis, pairs))
            for y in received:
                x = x + y
            stride *= ways
    return x


def body(start, inv_factor, partner, partner_face, elem_class, elem_face, load_map, trace_map):
    subs, _, _, rhs, half = start.shape
    elems = elem_class.shape[1]
    classes = load_map.shape[0]
    kept = len(KEPT)
    count = start.size // rhs * lax.axis_size("slab") * lax.axis_size("sub")
    smem = pl.BlockSpec(memory_space=pltpu.SMEM)
    vmem = pl.BlockSpec(memory_space=pltpu.VMEM)
    hbm = pl.BlockSpec(memory_space=pl.ANY)

    def scratch(sums):
        return [
            pltpu.VMEM((sums, half, 2 * half), F32),
            pltpu.VMEM((classes, half, 2 * half), BF16),
            pltpu.VMEM((classes, 2 * half, 2 * half), BF16),
            pltpu.VMEM((subs * elems, 2, half, half), BF16),
            pltpu.SemaphoreType.DMA((subs * elems,)),
            pltpu.SMEM((subs * elems + 1,), jnp.int32),
            pltpu.VMEM((GROUP, half, 2 * half), F32),
        ]

    load = jax.ShapeDtypeStruct((subs, half + rhs + 16, 2 * half), F32)
    to_sub, to_slab = pl.pallas_call(
        compose_sent,
        out_shape=(load, load),
        in_specs=[smem, smem, smem, hbm, vmem, vmem, vmem],
        out_specs=(vmem, vmem),
        scratch_shapes=scratch(2 * subs),
        name="compose_sent",
        cost_estimate=pl.CostEstimate(flops=10**9, bytes_accessed=4 * 10**6, transcendentals=0),
    )(elem_face, elem_class, partner, inv_factor, load_map, trace_map, start)

    def shifted(x, axis, up):
        last = lax.axis_size(axis) - 1
        return lax.ppermute(x, axis, [(i, i + 1) if up else (i + 1, i) for i in range(last)])

    from_slab = shifted(to_slab, "slab", False)
    from_sub = shifted(to_sub, "sub", False)

    square = jax.ShapeDtypeStruct((subs * kept, 2 * half, 2 * half), BF16)
    high, low = pl.pallas_call(
        compose_kept,
        out_shape=(square, square),
        in_specs=[smem, smem, hbm, vmem, vmem],
        out_specs=(vmem, vmem),
        scratch_shapes=scratch(subs * kept),
        name="compose_kept",
        cost_estimate=pl.CostEstimate(flops=2 * 10**9, bytes_accessed=8 * 10**6, transcendentals=0),
    )(elem_face, elem_class, inv_factor, load_map, trace_map)

    size = (ITERS + 1) * rhs
    back = jax.ShapeDtypeStruct((subs, ITERS * rhs, 2 * half), F32)
    gram, blocks, ret_sub, ret_slab = pl.pallas_call(
        krylov,
        out_shape=(
            jax.ShapeDtypeStruct((2 * rhs, 128), F32),
            jax.ShapeDtypeStruct((subs * kept, size, 2 * half), F32),
            back,
            back,
        ),
        in_specs=[smem, smem, vmem, vmem, vmem, vmem, vmem],
        out_specs=(vmem, vmem, vmem, vmem),
        scratch_shapes=[
            pltpu.VMEM((2 * subs, 2 * half, 2 * half), BF16),
            pltpu.VMEM((2 * subs, 2 * half, 2 * half), BF16),
            pltpu.VMEM((2 * subs, size, 2 * half), F32),
            pltpu.VMEM((subs * (kept + 2), rhs, 2 * half), F32),
        ],
        name="krylov",
    )(partner, partner_face, high, low, from_sub, from_slab, start)

    back_slab = shifted(ret_slab, "slab", True)
    back_sub = shifted(ret_sub, "sub", True)
    gram = summed(gram, ("sub", "slab"))

    return pl.pallas_call(
        functools.partial(finish, float(count)),
        out_shape=(
            jax.ShapeDtypeStruct(start.shape, F32),
            jax.ShapeDtypeStruct((ITERS, ITERS + 1, rhs, rhs), F32),
        ),
        in_specs=[vmem] * 5,
        out_specs=(vmem, vmem),
        scratch_shapes=[pltpu.VMEM((128, 128), F32), pltpu.VMEM((128, 128), F32)],
        name="finish",
    )(gram, blocks, back_sub, back_slab, start)


def solution(mesh):
    placed = (
        P(("slab", "sub"), None, None, None, None),
        P(("slab", "sub"), None, None, None),
        P(("slab", "sub"), None),
        P(("slab", "sub"), None),
        P(("slab", "sub"), None),
        P(("slab", "sub"), None),
        P(),
        P(),
    )
    return jax.shard_map(
        body,
        mesh=mesh,
        in_specs=placed,
        out_specs=(P(("slab", "sub"), None, None, None, None), P()),
        check_vma=False,
    )
```

```python
import functools

import jax
import jax.numpy as jnp
from jax import lax
from jax.experimental import pallas as pl
from jax.experimental.pallas import tpu as pltpu
from jax.sharding import PartitionSpec as P


ITERS = 4
STEP_SCALE = 2.0**-8
INNER = (0, 1)
SHARED = (3, 5)
SENT = (2, 4)
GROUP = 4
ROWS = ((4, 1, 0), (3, 2))

F32 = jnp.float32
BF16 = jnp.bfloat16
HIGHEST = lax.Precision.HIGHEST
PARAMS = pltpu.CompilerParams(vmem_limit_bytes=24 * 2**20)


def dot(a, b, transposed=False, precision=None):
    dims = (((1,), (1 if transposed else 0,)), ((), ()))
    return lax.dot_general(a, b, dims, precision=precision, preferred_element_type=F32)


def two_parts(x):
    high = x.astype(BF16)
    return high, (x - high.astype(F32)).astype(BF16)


def doubled(x):
    return jnp.concatenate(two_parts(x), axis=0)


def embedded(real, imag):
    return jnp.concatenate(
        [jnp.concatenate([real, -imag], axis=1), jnp.concatenate([imag, real], axis=1)], axis=0
    )


def compose(faces, face_ref, class_ref, held, first_ref, last_ref, sum_ref, lists, part):
    ids, kinds, places = lists
    subs, elems = face_ref.shape
    half = held.shape[2]
    total = jnp.int32(0)
    for s in range(subs):
        for e in range(elems):
            face = face_ref[s, e]
            place = jnp.int32(s * len(faces))
            hit = face == faces[0]
            for i in range(1, len(faces)):
                hit = hit | (face == faces[i])
                place = jnp.where(face == faces[i], s * len(faces) + i, place)
            ids[total] = s * elems + e
            kinds[total] = class_ref[s, e]
            places[total] = place
            total = total + hit.astype(jnp.int32)
    sum_ref[...] = jnp.zeros_like(sum_ref)

    def group(g, carry):
        where = [jnp.minimum(g * GROUP + u, total - 1) for u in range(GROUP)]
        for u in range(GROUP):
            kind = kinds[where[u]]
            wide = embedded(held[ids[where[u]], 0], held[ids[where[u]], 1])
            out = dot(first_ref[kind], wide, True)
            out = dot(doubled(out), wide)
            out = dot(doubled(out[:half] + out[half:]), last_ref[kind], True)
            part[u] = out[:half] + out[half:]
        for u in range(GROUP):
            at = places[where[u]]
            sum_ref[at] = sum_ref[at] + jnp.where(g * GROUP + u < total, part[u], 0.0)
        return carry

    lax.fori_loop(0, (total + GROUP - 1) // GROUP, group, 0)


def pack(out_ref, sum_ref, start_of, partner_ref, face, subs):
    half = sum_ref.shape[1]
    for s in range(subs):
        real, imag = start_of(s)
        rhs = real.shape[0]
        out_ref[s, :half] = sum_ref[s]
        out_ref[s, half : half + rhs, :half] = real
        out_ref[s, half : half + rhs, half:] = imag
        partner = partner_ref[s, face]
        there = (partner >= 0).astype(F32)
        local = jnp.where(partner >= 0, partner % subs, 0).astype(F32)
        out_ref[s, half + rhs : half + rhs + 8] = jnp.full((8, 2 * half), local, F32)
        out_ref[s, half + rhs + 8 : half + rhs + 16] = jnp.full((8, 2 * half), there, F32)


def compose_slab(face_hbm, class_hbm, partner_hbm, inv_ref, load_ref, trace_ref, start_ref,
                 out_ref, held, first_ref, last_ref, sum_ref, part, ids, kinds, places,
                 load, trace, rows, face_ref, class_ref, partner_ref, sems):
    subs = face_ref.shape[0]
    half = load_ref.shape[2]
    pieces = sems.shape[0] - 6
    step = inv_ref.shape[0] // pieces
    copies = [
        pltpu.make_async_copy(load_ref, load, sems.at[0]),
        pltpu.make_async_copy(trace_ref, trace, sems.at[1]),
        pltpu.make_async_copy(start_ref.at[:, SENT[1]], rows, sems.at[2]),
    ]
    for i, (source, place) in enumerate(
        ((face_hbm, face_ref), (class_hbm, class_ref), (partner_hbm, partner_ref))
    ):
        copies.append(pltpu.make_async_copy(source, place, sems.at[3 + i]))
    for i in range(pieces):
        span = pl.ds(i * step, step)
        copies.append(pltpu.make_async_copy(inv_ref.at[span], held.at[span], sems.at[6 + i]))
    for copy in copies:
        copy.start()
    copies[0].wait()
    copies[1].wait()
    for c in range(load_ref.shape[0]):
        for x in range(2):
            first_ref[c, :, x * half : (x + 1) * half] = load[c, x].astype(F32).T.astype(BF16)
        last_ref[c] = embedded(trace[c, 0], trace[c, 1])
    for copy in copies[2:]:
        copy.wait()
    compose(SENT[1:], face_ref, class_ref, held, first_ref, last_ref, sum_ref,
            (ids, kinds, places), part)
    pack(out_ref, sum_ref, lambda s: (rows[s, 0], rows[s, 1]), partner_ref, SENT[1], subs)


def compose_sub(face_ref, class_ref, partner_ref, held, first_ref, last_ref, start_ref,
                out_ref, sum_ref, part, ids, kinds, places):
    subs = face_ref.shape[0]
    compose(SENT[:1], face_ref, class_ref, held, first_ref, last_ref, sum_ref,
            (ids, kinds, places), part)
    pack(out_ref, sum_ref, lambda s: (start_ref[s, SENT[0], 0], start_ref[s, SENT[0], 1]),
         partner_ref, SENT[0], subs)


def spread(rows):
    half = rows.shape[0]
    lower = jnp.concatenate([-rows[:, half:], rows[:, :half]], axis=1)
    return two_parts(jnp.concatenate([rows, lower], axis=0))


def leaving(high, low, x, wide_high, wide_low):
    rhs = x.shape[0]
    both = dot(jnp.concatenate([high, low], axis=0), wide_high)
    return (both[:rhs] + both[rhs:] + dot(high, wide_low) - x) * STEP_SCALE


def products(pairs):
    total = None
    for high, low in pairs:
        both = jnp.concatenate([high, low], axis=0)
        term = dot(both, both, True)
        total = term if total is None else total + term
    size = total.shape[0] // 2
    return (total[:size, :size] + total[size:, size:]) + (total[:size, size:] + total[size:, :size])


def compose_kept(face_ref, class_ref, partner_ref, partner_face_ref, held, first_ref, last_ref,
                 start_ref, wide_high, wide_low, rows_high, rows_low, gram_ref,
                 sum_ref, part, ids, kinds, places, inner_high, inner_low, now_ref, out_ref):
    subs, _, _, rhs, _ = start_ref.shape
    faces = INNER + SHARED
    inner = len(INNER)
    compose(faces, face_ref, class_ref, held, first_ref, last_ref, sum_ref,
            (ids, kinds, places), part)
    for s in range(subs):
        for i in range(len(faces)):
            high, low = spread(sum_ref[s * len(faces) + i])
            if i < inner:
                inner_high[s * inner + i] = high
                inner_low[s * inner + i] = low
            else:
                at = (i - inner) * subs + s
                wide_high[at] = high
                wide_low[at] = low
    slots = subs * inner
    for s in range(subs):
        for f in INNER:
            value = jnp.concatenate([start_ref[s, f, 0], start_ref[s, f, 1]], axis=1)
            now_ref[s * inner + f] = value
            high, low = two_parts(value)
            rows_high[s * inner + f, :rhs] = high
            rows_low[s * inner + f, :rhs] = low
    for k in range(ITERS):
        now = slice(k * rhs, (k + 1) * rhs)
        later = slice((k + 1) * rhs, (k + 2) * rhs)
        for at in range(slots):
            out_ref[at] = leaving(rows_high[at, now], rows_low[at, now], now_ref[at],
                                  inner_high[at], inner_low[at])
        for s in range(subs):
            for f in INNER:
                local = partner_ref[s, f] % subs * inner + partner_face_ref[s, f]
                value = out_ref[0]
                for p in range(1, slots):
                    value = jnp.where(local == p, out_ref[p], value)
                now_ref[s * inner + f] = value
                high, low = two_parts(value)
                rows_high[s * inner + f, later] = high
                rows_low[s * inner + f, later] = low
    size = (ITERS + 1) * rhs
    gram_ref[:, :size] = products([(rows_high[at], rows_low[at]) for at in range(slots)])


def krylov(partner_ref, wide_high, wide_low, from_sub_ref, from_slab_ref, start_ref, inner_ref,
           gram_ref, rows_high, rows_low, to_sub_ref, to_slab_ref,
           far_wide_high, far_wide_low, far_high, far_low, now_ref, out_ref):
    subs, _, _, rhs, half = start_ref.shape
    own = 2 * subs
    sources = (from_sub_ref, from_slab_ref)
    targets = (to_sub_ref, to_slab_ref)

    for d in range(2):
        for s in range(subs):
            at = d * subs + s
            face = SHARED[d]
            far_wide_high[at], far_wide_low[at] = spread(sources[d][s, :half])
            value = jnp.concatenate([start_ref[s, face, 0], start_ref[s, face, 1]], axis=1)
            now_ref[at] = value
            rows_high[at, :rhs], rows_low[at, :rhs] = two_parts(value)
            value = sources[d][s, half : half + rhs]
            now_ref[own + at] = value
            far_high[at, :rhs], far_low[at, :rhs] = two_parts(value)

    for k in range(ITERS):
        now = slice(k * rhs, (k + 1) * rhs)
        later = slice((k + 1) * rhs, (k + 2) * rhs)
        for at in range(own):
            out_ref[at] = leaving(rows_high[at, now], rows_low[at, now], now_ref[at],
                                  wide_high[at], wide_low[at])
            out_ref[own + at] = leaving(far_high[at, now], far_low[at, now], now_ref[own + at],
                                        far_wide_high[at], far_wide_low[at])
        for d in range(2):
            for s in range(subs):
                at = d * subs + s
                partner = partner_ref[s, SHARED[d]]
                local = partner % subs
                value = out_ref[own + d * subs]
                for p in range(1, subs):
                    value = jnp.where(local == p, out_ref[own + d * subs + p], value)
                value = jnp.where(partner >= 0, value, 0.0)
                now_ref[at] = value
                rows_high[at, later], rows_low[at, later] = two_parts(value)
                local = sources[d][s, half + rhs : half + rhs + 1]
                there = sources[d][s, half + rhs + 8 : half + rhs + 9]
                value = out_ref[d * subs]
                for p in range(1, subs):
                    value = jnp.where(local > p - 0.5, out_ref[d * subs + p], value)
                value = jnp.where(there > 0.5, value, 0.0)
                now_ref[own + at] = value
                far_high[at, later], far_low[at, later] = two_parts(value)
                targets[d][s, now] = value

    size = (ITERS + 1) * rhs
    total = inner_ref[:, :size] + products(
        [(rows_high[at], rows_low[at]) for at in range(own)]
        + [(far_high[at], far_low[at]) for at in range(own)]
    )
    alone = []
    for face in SENT:
        for s in range(subs):
            share = jnp.where(partner_ref[s, face] < 0, 1.0, 0.0)
            rows = jnp.concatenate([start_ref[s, face, 0], start_ref[s, face, 1]], axis=1)
            alone.append(two_parts(rows * share))
    first = total[:rhs, :rhs] + products(alone)

    gram_ref[...] = jnp.zeros_like(gram_ref)
    for row, blocks in enumerate(ROWS):
        lane = 0
        for i in blocks:
            width = (i + 1) * rhs
            piece = first if i == 0 else total[i * rhs : (i + 1) * rhs, :width]
            gram_ref[row * rhs : (row + 1) * rhs, lane : lane + width] = piece
            lane += width


def finish(count, gram_ref, inner_high, inner_low, rows_high, rows_low, back_sub_ref,
           back_slab_ref, start_ref, last_ref, hess_ref, upper_ref, inverse_ref, back_high, back_low):
    subs, _, _, rhs, half = start_ref.shape
    size = (ITERS + 1) * rhs
    lanes = 128
    for d, back_ref in enumerate((back_sub_ref, back_slab_ref)):
        for s in range(subs):
            at = d * subs + s
            first = jnp.concatenate([start_ref[s, SENT[d], 0], start_ref[s, SENT[d], 1]], axis=1)
            back_high[at, :rhs], back_low[at, :rhs] = two_parts(first)
            back_high[at, rhs:], back_low[at, rhs:] = two_parts(back_ref[s])

    upper_ref[...] = jnp.zeros_like(upper_ref)
    for row, blocks in enumerate(ROWS):
        lane = 0
        for i in blocks:
            width = (i + 1) * rhs
            upper_ref[i * rhs : (i + 1) * rhs, :width] = (
                gram_ref[row * rhs : (row + 1) * rhs, lane : lane + width] / count
            )
            lane += width
    lower = upper_ref[...]
    down = lax.broadcasted_iota(jnp.int32, (lanes, lanes), 0)
    across = lax.broadcasted_iota(jnp.int32, (lanes, lanes), 1)
    full = jnp.where(down >= across, lower, lower.T)

    blocks = size // 8
    work = [full[8 * i : 8 * i + 8] for i in range(blocks)]
    side = [
        (down[8 * i : 8 * i + 8] == across[8 * i : 8 * i + 8]).astype(F32) for i in range(blocks)
    ]
    sub_row = lax.broadcasted_iota(jnp.int32, (8, lanes), 0)

    def spread_row(x, r):
        return jnp.broadcast_to(x[r : r + 1], (8, lanes))

    for i in range(blocks):
        columns = {
            m: [jnp.broadcast_to(work[m][:, 8 * i + q : 8 * i + q + 1], (8, lanes)) for q in range(8)]
            for m in range(i, blocks)
        }
        own = list(columns[i])
        row, other = work[i], side[i]
        for r in range(8):
            pivot = spread_row(own[r], r)
            root = lax.rsqrt(pivot)
            scale = 1.0 / pivot
            chosen = sub_row == r
            factor = own[r]
            top, rest = spread_row(row, r), spread_row(other, r)
            j = 8 * i + r
            upper_ref[j : j + 1, :] = (top * root)[:1]
            inverse_ref[j : j + 1, :] = (rest * root)[:1]

            def cleared(x, x_row):
                x_row = x_row * scale
                return jnp.where(chosen, x_row, x - factor * x_row)

            row, other = cleared(row, top), cleared(other, rest)
            for q in range(r + 1, 8):
                own[q] = cleared(own[q], spread_row(own[q], r))
        tops = [spread_row(row, q) for q in range(8)]
        rests = [spread_row(other, q) for q in range(8)]
        for m in range(i + 1, blocks):
            terms = [columns[m][q] * tops[q] for q in range(8)]
            while len(terms) > 1:
                terms = [terms[q] + terms[q + 1] for q in range(0, len(terms), 2)]
            work[m] = work[m] - terms[0]
            terms = [columns[m][q] * rests[q] for q in range(8)]
            while len(terms) > 1:
                terms = [terms[q] + terms[q + 1] for q in range(0, len(terms), 2)]
            side[m] = side[m] - terms[0]
    upper_ref[size:, :] = jnp.zeros((lanes - size, lanes), F32)
    inverse_ref[size:, :] = jnp.zeros((lanes - size, lanes), F32)

    upper = jnp.where(down <= across, upper_ref[...], 0.0)
    inverse = jnp.where(down >= across, inverse_ref[...], 0.0)
    mix = inverse[ITERS * rhs : size, :size]
    mix_high, mix_low = two_parts(mix)
    mix_both = jnp.concatenate([mix_high, mix_low], axis=0)

    def put(s, face, high, low):
        value = dot(mix_both, high)
        value = value[:rhs] + value[rhs:] + dot(mix_high, low)
        last_ref[s, face, 0] = value[:, :half]
        last_ref[s, face, 1] = value[:, half:]

    for s in range(subs):
        for f in INNER:
            at = s * len(INNER) + f
            put(s, f, inner_high[at], inner_low[at])
        for d in range(2):
            at = d * subs + s
            put(s, SHARED[d], rows_high[at], rows_low[at])
            put(s, SENT[d], back_high[at], back_low[at])

    shifted = jnp.concatenate([upper[:, rhs:], jnp.zeros((lanes, rhs), F32)], axis=1)
    moved = dot(shifted, inverse, True, HIGHEST) * (1.0 / STEP_SCALE)
    unit = (down[:rhs, :rhs] == across[:rhs, :rhs]).astype(F32)
    for k in range(ITERS):
        for j in range(ITERS + 1):
            if j > k + 1:
                hess_ref[k, j] = jnp.zeros((rhs, rhs), F32)
                continue
            block = moved[j * rhs : (j + 1) * rhs, k * rhs : (k + 1) * rhs]
            block = block if (j + k) % 2 else -block
            hess_ref[k, j] = block + unit if j == k else block


def summed(x, axes):
    for axis in axes:
        count, stride = lax.axis_size(axis), 1
        while stride < count:
            rest = count // stride
            ways = next(p for p in range(2, rest + 1) if rest % p == 0)
            received = []
            for d in range(1, ways):
                pairs = []
                for i in range(count):
                    digit = (i // stride) % ways
                    pairs.append((i, i + ((digit + d) % ways - digit) * stride))
                received.append(lax.ppermute(x, axis, pairs))
            for y in received:
                x = x + y
            stride *= ways
    return x


def body(start, inv_factor, partner, partner_face, elem_class, elem_face, load_map, trace_map):
    subs, _, _, rhs, half = start.shape
    elems = elem_class.shape[1]
    classes = load_map.shape[0]
    count = start.size // rhs * lax.axis_size("slab") * lax.axis_size("sub")
    size = (ITERS + 1) * rhs
    full = 2 * half
    smem = pl.BlockSpec(memory_space=pltpu.SMEM)
    vmem = pl.BlockSpec(memory_space=pltpu.VMEM)
    hbm = pl.BlockSpec(memory_space=pltpu.HBM)

    def shape(*dims, dtype=F32):
        return jax.ShapeDtypeStruct(dims, dtype)

    def scratch(sums):
        return [
            pltpu.VMEM((sums, half, full), F32),
            pltpu.VMEM((GROUP, half, full), F32),
            pltpu.SMEM((subs * elems + 1,), jnp.int32),
            pltpu.SMEM((subs * elems + 1,), jnp.int32),
            pltpu.SMEM((subs * elems + 1,), jnp.int32),
        ]

    def call(kernel, out_shape, in_specs, scratch_shapes):
        return pl.pallas_call(
            kernel,
            out_shape=out_shape,
            in_specs=in_specs,
            out_specs=(vmem,) * len(out_shape),
            scratch_shapes=scratch_shapes,
            compiler_params=PARAMS,
            cost_estimate=pl.CostEstimate(
                flops=2 * 10**9, bytes_accessed=4 * 10**6, transcendentals=0
            ),
        )

    def shifted(x, axis, up):
        last = lax.axis_size(axis) - 1
        return lax.ppermute(x, axis, [(i, i + 1) if up else (i + 1, i) for i in range(last)])

    load = shape(subs, half + rhs + 16, full)
    far = [
        pltpu.with_memory_space_constraint(x, pltpu.HBM)
        for x in (elem_face, elem_class, partner, inv_factor, load_map, trace_map, start)
    ]
    to_slab, held, first, last = call(
        compose_slab,
        (load, shape(*inv_factor.shape, dtype=BF16), shape(classes, half, full, dtype=BF16),
         shape(classes, full, full, dtype=BF16)),
        [hbm] * 7,
        scratch(subs) + [
            pltpu.VMEM(load_map.shape, BF16),
            pltpu.VMEM(trace_map.shape, BF16),
            pltpu.VMEM((subs, 2, rhs, half), F32),
            pltpu.SMEM(elem_face.shape, jnp.int32),
            pltpu.SMEM(elem_class.shape, jnp.int32),
            pltpu.SMEM(partner.shape, jnp.int32),
            pltpu.SemaphoreType.DMA((6 + 4,)),
        ],
    )(*far)
    from_slab = shifted(to_slab, "slab", False)

    (to_sub,) = call(
        compose_sub, (load,), [smem, smem, smem] + [vmem] * 4, scratch(subs)
    )(elem_face, elem_class, partner, held, first, last, start)
    from_sub = shifted(to_sub, "sub", False)

    slots = 2 * subs
    square = shape(slots, full, full, dtype=BF16)
    rows = shape(slots, size, full, dtype=BF16)
    wide_high, wide_low, inner_high, inner_low, inner_gram = call(
        compose_kept,
        (square, square, rows, rows, shape(size, 128)),
        [smem, smem, smem, smem] + [vmem] * 4,
        scratch(2 * slots) + [
            pltpu.VMEM((slots, full, full), BF16),
            pltpu.VMEM((slots, full, full), BF16),
            pltpu.VMEM((slots, rhs, full), F32),
            pltpu.VMEM((slots, rhs, full), F32),
        ],
    )(elem_face, elem_class, partner, partner_face, held, first, last, start)

    back = shape(subs, ITERS * rhs, full)
    gram, rows_high, rows_low, ret_sub, ret_slab = call(
        krylov,
        (shape(2 * rhs, 128), rows, rows, back, back),
        [smem] + [vmem] * 6,
        [
            pltpu.VMEM((slots, full, full), BF16),
            pltpu.VMEM((slots, full, full), BF16),
            pltpu.VMEM((slots, size, full), BF16),
            pltpu.VMEM((slots, size, full), BF16),
            pltpu.VMEM((2 * slots, rhs, full), F32),
            pltpu.VMEM((2 * slots, rhs, full), F32),
        ],
    )(partner, wide_high, wide_low, from_sub, from_slab, start, inner_gram)

    back_slab = shifted(ret_slab, "slab", True)
    back_sub = shifted(ret_sub, "sub", True)
    gram = summed(gram, ("sub", "slab"))

    return call(
        functools.partial(finish, float(count)),
        (shape(*start.shape), shape(ITERS, ITERS + 1, rhs, rhs)),
        [vmem] * 8,
        [
            pltpu.VMEM((128, 128), F32),
            pltpu.VMEM((128, 128), F32),
            pltpu.VMEM((slots, size, full), BF16),
            pltpu.VMEM((slots, size, full), BF16),
        ],
    )(gram, inner_high, inner_low, rows_high, rows_low, back_sub, back_slab, start)


def solution(mesh):
    placed = (
        P(("slab", "sub"), None, None, None, None),
        P(("slab", "sub"), None, None, None),
        P(("slab", "sub"), None),
        P(("slab", "sub"), None),
        P(("slab", "sub"), None),
        P(("slab", "sub"), None),
        P(),
        P(),
    )

    return jax.shard_map(
        body,
        mesh=mesh,
        in_specs=placed,
        out_specs=(P(("slab", "sub"), None, None, None, None), P()),
        check_vma=False,
    )
```

```python
import functools

import jax
import jax.numpy as jnp
from jax import lax
from jax.experimental import pallas as pl
from jax.experimental.pallas import tpu as pltpu
from jax.sharding import PartitionSpec as P


ITERS = 4
STEP_SCALE = 2.0**-8
INNER = (0, 1)
SHARED = (3, 5)
SENT = (2, 4)
GROUP = 8
LEAST = 2
ROWS = ((4, 1, 0), (3, 2))

F32 = jnp.float32
BF16 = jnp.bfloat16
HIGHEST = lax.Precision.HIGHEST
PARAMS = pltpu.CompilerParams(vmem_limit_bytes=24 * 2**20)


def dot(a, b, transposed=False, precision=None):
    dims = (((1,), (1 if transposed else 0,)), ((), ()))
    return lax.dot_general(a, b, dims, precision=precision, preferred_element_type=F32)


def two_parts(x):
    high = x.astype(BF16)
    return high, (x - high.astype(F32)).astype(BF16)


def doubled(x):
    return jnp.concatenate(two_parts(x), axis=0)


def embedded(real, imag):
    return jnp.concatenate(
        [jnp.concatenate([real, -imag], axis=1), jnp.concatenate([imag, real], axis=1)], axis=0
    )


def listed(face_ref, class_ref, order):
    subs, elems = face_ref.shape
    front, back = jnp.int32(0), jnp.int32(subs * elems - 1)
    for s in range(subs):
        for e in range(elems):
            face = face_ref[s, e]
            hit = (face == SENT[0]) | (face == SENT[1])
            order[jnp.where(hit, front, back)] = (
                (s * elems + e) * 4096 + (face * subs + s) * 64 + class_ref[s, e]
            )
            hit = hit.astype(jnp.int32)
            front, back = front + hit, back - 1 + hit
    return front


def groups(count):
    return (count + GROUP - 1) // GROUP


def stop_of(sent):
    return jnp.maximum(groups(sent), LEAST)


def compose(span, total, held, first_ref, last_ref, sum_ref, order, part):
    half = held.shape[2]
    sum_ref[...] = jnp.zeros_like(sum_ref)

    def group(g, carry):
        words = [order[jnp.minimum(g * GROUP + u, total - 1)] for u in range(GROUP)]
        for u in range(GROUP):
            kind = words[u] & 63
            e = lax.shift_right_logical(words[u], 12)
            wide = embedded(held[e, 0], held[e, 1])
            out = dot(first_ref[kind], wide, True)
            out = dot(doubled(out), wide)
            out = dot(doubled(out[:half] + out[half:]), last_ref[kind])
            part[u] = out[:half] + out[half:]
        for u in range(GROUP):
            at = lax.shift_right_logical(words[u], 6) & 63
            sum_ref[at] = sum_ref[at] + jnp.where(g * GROUP + u < total, part[u], 0.0)
        return carry

    lax.fori_loop(span[0], span[1], group, 0)


def pack(out_ref, operator_of, start_of, partner_ref, face, subs):
    for s in range(subs):
        real, imag = start_of(s)
        rhs, half = real.shape
        out_ref[s, :half] = operator_of(s)
        out_ref[s, half : half + rhs, :half] = real
        out_ref[s, half : half + rhs, half:] = imag
        partner = partner_ref[s, face]
        there = (partner >= 0).astype(F32)
        local = jnp.where(partner >= 0, partner % subs, 0).astype(F32)
        out_ref[s, half + rhs : half + rhs + 8] = jnp.full((8, 2 * half), local, F32)
        out_ref[s, half + rhs + 8 : half + rhs + 16] = jnp.full((8, 2 * half), there, F32)


def compose_sent(face_hbm, class_hbm, partner_hbm, inv_ref, load_ref, trace_ref, start_ref,
                 to_sub, to_slab, held, first_ref, last_ref, sum_ref, part, order,
                 load, trace, sub_rows, slab_rows, face_ref, class_ref, partner_ref, sems):
    subs = face_ref.shape[0]
    half = load_ref.shape[2]
    copies = []
    for source, place in (
        (load_ref, load),
        (trace_ref, trace),
        (face_hbm, face_ref),
        (class_hbm, class_ref),
        (start_ref.at[:, SENT[0]], sub_rows),
        (start_ref.at[:, SENT[1]], slab_rows),
        (partner_hbm, partner_ref),
    ):
        copies.append(pltpu.make_async_copy(source, place, sems.at[len(copies)]))
    small = len(copies)
    step = inv_ref.shape[0] // (sems.shape[0] - small)
    for i in range(sems.shape[0] - small):
        span = pl.ds(i * step, step)
        copies.append(
            pltpu.make_async_copy(inv_ref.at[span], held.at[span], sems.at[small + i])
        )
    for copy in copies:
        copy.start()
    for copy in copies[:2]:
        copy.wait()
    for c in range(load_ref.shape[0]):
        for x in range(2):
            first_ref[c, :, x * half : (x + 1) * half] = load[c, x].astype(F32).T.astype(BF16)
        real, imag = [trace[c, x].astype(F32).T.astype(BF16) for x in range(2)]
        last_ref[c] = embedded(real, -imag)
    for copy in copies[2:small]:
        copy.wait()
    stop = stop_of(listed(face_ref, class_ref, order))
    for copy in copies[small:]:
        copy.wait()
    compose((0, stop), held.shape[0], held, first_ref, last_ref, sum_ref, order, part)
    for out_ref, rows, face in ((to_sub, sub_rows, SENT[0]), (to_slab, slab_rows, SENT[1])):
        pack(out_ref, lambda s: sum_ref[face * subs + s], lambda s: (rows[s, 0], rows[s, 1]),
             partner_ref, face, subs)


def spread(rows):
    half = rows.shape[0]
    lower = jnp.concatenate([-rows[:, half:], rows[:, :half]], axis=1)
    return two_parts(jnp.concatenate([rows, lower], axis=0))


def leaving(high, low, x, wide_high, wide_low):
    rhs = x.shape[0]
    both = dot(jnp.concatenate([high, low], axis=0), wide_high)
    return (both[:rhs] + both[rhs:] + dot(high, wide_low) - x) * STEP_SCALE


def products(pairs):
    total = None
    for high, low in pairs:
        both = jnp.concatenate([high, low], axis=0)
        term = dot(both, both, True)
        total = term if total is None else total + term
    size = total.shape[0] // 2
    return (total[:size, :size] + total[size:, size:]) + (total[:size, size:] + total[size:, :size])


def compose_kept(face_ref, class_ref, partner_ref, partner_face_ref, held, first_ref, last_ref,
                 start_ref, sent_sum, wide_high, wide_low, rows_high, rows_low, gram_ref,
                 sum_ref, part, order, inner_high, inner_low, now_ref, out_ref):
    subs, _, _, rhs, _ = start_ref.shape
    faces = INNER + SHARED
    inner = len(INNER)
    stop = stop_of(listed(face_ref, class_ref, order))
    total = held.shape[0]
    compose((stop, groups(total)), total, held, first_ref, last_ref, sum_ref, order, part)
    for s in range(subs):
        for i, face in enumerate(faces):
            at = face * subs + s
            high, low = spread(sent_sum[at] + sum_ref[at])
            if i < inner:
                inner_high[s * inner + i] = high
                inner_low[s * inner + i] = low
            else:
                at = (i - inner) * subs + s
                wide_high[at] = high
                wide_low[at] = low
    slots = subs * inner
    for s in range(subs):
        for f in INNER:
            value = jnp.concatenate([start_ref[s, f, 0], start_ref[s, f, 1]], axis=1)
            now_ref[s * inner + f] = value
            high, low = two_parts(value)
            rows_high[s * inner + f, :rhs] = high
            rows_low[s * inner + f, :rhs] = low
    for k in range(ITERS):
        now = slice(k * rhs, (k + 1) * rhs)
        later = slice((k + 1) * rhs, (k + 2) * rhs)
        for at in range(slots):
            out_ref[at] = leaving(rows_high[at, now], rows_low[at, now], now_ref[at],
                                  inner_high[at], inner_low[at])
        for s in range(subs):
            for f in INNER:
                local = partner_ref[s, f] % subs * inner + partner_face_ref[s, f]
                value = out_ref[0]
                for p in range(1, slots):
                    value = jnp.where(local == p, out_ref[p], value)
                now_ref[s * inner + f] = value
                high, low = two_parts(value)
                rows_high[s * inner + f, later] = high
                rows_low[s * inner + f, later] = low
    size = (ITERS + 1) * rhs
    gram_ref[:, :size] = products([(rows_high[at], rows_low[at]) for at in range(slots)])


def krylov(partner_ref, wide_high, wide_low, from_sub_ref, from_slab_ref, start_ref, inner_ref,
           gram_ref, rows_high, rows_low, to_sub_ref, to_slab_ref,
           far_wide_high, far_wide_low, far_high, far_low, now_ref, out_ref):
    subs, _, _, rhs, half = start_ref.shape
    own = 2 * subs
    sources = (from_sub_ref, from_slab_ref)
    targets = (to_sub_ref, to_slab_ref)

    for d in range(2):
        for s in range(subs):
            at = d * subs + s
            face = SHARED[d]
            far_wide_high[at], far_wide_low[at] = spread(sources[d][s, :half])
            value = jnp.concatenate([start_ref[s, face, 0], start_ref[s, face, 1]], axis=1)
            now_ref[at] = value
            rows_high[at, :rhs], rows_low[at, :rhs] = two_parts(value)
            value = sources[d][s, half : half + rhs]
            now_ref[own + at] = value
            far_high[at, :rhs], far_low[at, :rhs] = two_parts(value)

    for k in range(ITERS):
        now = slice(k * rhs, (k + 1) * rhs)
        later = slice((k + 1) * rhs, (k + 2) * rhs)
        for at in range(own):
            out_ref[at] = leaving(rows_high[at, now], rows_low[at, now], now_ref[at],
                                  wide_high[at], wide_low[at])
            out_ref[own + at] = leaving(far_high[at, now], far_low[at, now], now_ref[own + at],
                                        far_wide_high[at], far_wide_low[at])
        for d in range(2):
            for s in range(subs):
                at = d * subs + s
                partner = partner_ref[s, SHARED[d]]
                local = partner % subs
                value = out_ref[own + d * subs]
                for p in range(1, subs):
                    value = jnp.where(local == p, out_ref[own + d * subs + p], value)
                value = jnp.where(partner >= 0, value, 0.0)
                now_ref[at] = value
                rows_high[at, later], rows_low[at, later] = two_parts(value)
                local = sources[d][s, half + rhs : half + rhs + 1]
                there = sources[d][s, half + rhs + 8 : half + rhs + 9]
                value = out_ref[d * subs]
                for p in range(1, subs):
                    value = jnp.where(local > p - 0.5, out_ref[d * subs + p], value)
                value = jnp.where(there > 0.5, value, 0.0)
                now_ref[own + at] = value
                far_high[at, later], far_low[at, later] = two_parts(value)
                targets[d][s, now] = value

    size = (ITERS + 1) * rhs
    total = inner_ref[:, :size] + products(
        [(rows_high[at], rows_low[at]) for at in range(own)]
        + [(far_high[at], far_low[at]) for at in range(own)]
    )
    alone = []
    for face in SENT:
        for s in range(subs):
            share = jnp.where(partner_ref[s, face] < 0, 1.0, 0.0)
            rows = jnp.concatenate([start_ref[s, face, 0], start_ref[s, face, 1]], axis=1)
            alone.append(two_parts(rows * share))
    first = total[:rhs, :rhs] + products(alone)

    gram_ref[...] = jnp.zeros_like(gram_ref)
    for row, blocks in enumerate(ROWS):
        lane = 0
        for i in blocks:
            width = (i + 1) * rhs
            piece = first if i == 0 else total[i * rhs : (i + 1) * rhs, :width]
            gram_ref[row * rhs : (row + 1) * rhs, lane : lane + width] = piece
            lane += width


def finish(count, gram_ref, inner_high, inner_low, rows_high, rows_low, back_sub_ref,
           back_slab_ref, start_ref, last_ref, hess_ref, upper_ref, inverse_ref, back_high, back_low):
    subs, _, _, rhs, half = start_ref.shape
    size = (ITERS + 1) * rhs
    lanes = 128
    for d, back_ref in enumerate((back_sub_ref, back_slab_ref)):
        for s in range(subs):
            at = d * subs + s
            first = jnp.concatenate([start_ref[s, SENT[d], 0], start_ref[s, SENT[d], 1]], axis=1)
            back_high[at, :rhs], back_low[at, :rhs] = two_parts(first)
            back_high[at, rhs:], back_low[at, rhs:] = two_parts(back_ref[s])

    upper_ref[...] = jnp.zeros_like(upper_ref)
    for row, blocks in enumerate(ROWS):
        lane = 0
        for i in blocks:
            width = (i + 1) * rhs
            upper_ref[i * rhs : (i + 1) * rhs, :width] = (
                gram_ref[row * rhs : (row + 1) * rhs, lane : lane + width] / count
            )
            lane += width
    lower = upper_ref[...]
    down = lax.broadcasted_iota(jnp.int32, (lanes, lanes), 0)
    across = lax.broadcasted_iota(jnp.int32, (lanes, lanes), 1)
    full = jnp.where(down >= across, lower, lower.T)

    blocks = size // 8
    work = [full[8 * i : 8 * i + 8] for i in range(blocks)]
    side = [
        (down[8 * i : 8 * i + 8] == across[8 * i : 8 * i + 8]).astype(F32) for i in range(blocks)
    ]
    sub_row = lax.broadcasted_iota(jnp.int32, (8, lanes), 0)

    def spread_row(x, r):
        return jnp.broadcast_to(x[r : r + 1], (8, lanes))

    for i in range(blocks):
        columns = {
            m: [jnp.broadcast_to(work[m][:, 8 * i + q : 8 * i + q + 1], (8, lanes)) for q in range(8)]
            for m in range(i, blocks)
        }
        own = list(columns[i])
        row, other = work[i], side[i]
        for r in range(8):
            pivot = spread_row(own[r], r)
            root = lax.rsqrt(pivot)
            scale = 1.0 / pivot
            chosen = sub_row == r
            factor = own[r]
            top, rest = spread_row(row, r), spread_row(other, r)
            j = 8 * i + r
            upper_ref[j : j + 1, :] = (top * root)[:1]
            inverse_ref[j : j + 1, :] = (rest * root)[:1]

            def cleared(x, x_row):
                x_row = x_row * scale
                return jnp.where(chosen, x_row, x - factor * x_row)

            row, other = cleared(row, top), cleared(other, rest)
            for q in range(r + 1, 8):
                own[q] = cleared(own[q], spread_row(own[q], r))
        tops = [spread_row(row, q) for q in range(8)]
        rests = [spread_row(other, q) for q in range(8)]
        for m in range(i + 1, blocks):
            terms = [columns[m][q] * tops[q] for q in range(8)]
            while len(terms) > 1:
                terms = [terms[q] + terms[q + 1] for q in range(0, len(terms), 2)]
            work[m] = work[m] - terms[0]
            terms = [columns[m][q] * rests[q] for q in range(8)]
            while len(terms) > 1:
                terms = [terms[q] + terms[q + 1] for q in range(0, len(terms), 2)]
            side[m] = side[m] - terms[0]
    upper_ref[size:, :] = jnp.zeros((lanes - size, lanes), F32)
    inverse_ref[size:, :] = jnp.zeros((lanes - size, lanes), F32)

    upper = jnp.where(down <= across, upper_ref[...], 0.0)
    inverse = jnp.where(down >= across, inverse_ref[...], 0.0)
    mix = inverse[ITERS * rhs : size, :size]
    mix_high, mix_low = two_parts(mix)
    mix_both = jnp.concatenate([mix_high, mix_low], axis=0)

    def put(s, face, high, low):
        value = dot(mix_both, high)
        value = value[:rhs] + value[rhs:] + dot(mix_high, low)
        last_ref[s, face, 0] = value[:, :half]
        last_ref[s, face, 1] = value[:, half:]

    for s in range(subs):
        for f in INNER:
            at = s * len(INNER) + f
            put(s, f, inner_high[at], inner_low[at])
        for d in range(2):
            at = d * subs + s
            put(s, SHARED[d], rows_high[at], rows_low[at])
            put(s, SENT[d], back_high[at], back_low[at])

    shifted = jnp.concatenate([upper[:, rhs:], jnp.zeros((lanes, rhs), F32)], axis=1)
    moved = dot(shifted, inverse, True, HIGHEST) * (1.0 / STEP_SCALE)
    unit = (down[:rhs, :rhs] == across[:rhs, :rhs]).astype(F32)
    for k in range(ITERS):
        for j in range(ITERS + 1):
            if j > k + 1:
                hess_ref[k, j] = jnp.zeros((rhs, rhs), F32)
                continue
            block = moved[j * rhs : (j + 1) * rhs, k * rhs : (k + 1) * rhs]
            block = block if (j + k) % 2 else -block
            hess_ref[k, j] = block + unit if j == k else block


def summed(x, axes):
    for axis in axes:
        count, stride = lax.axis_size(axis), 1
        while stride < count:
            rest = count // stride
            ways = next(p for p in range(2, rest + 1) if rest % p == 0)
            received = []
            for d in range(1, ways):
                pairs = []
                for i in range(count):
                    digit = (i // stride) % ways
                    pairs.append((i, i + ((digit + d) % ways - digit) * stride))
                received.append(lax.ppermute(x, axis, pairs))
            for y in received:
                x = x + y
            stride *= ways
    return x


def body(start, inv_factor, partner, partner_face, elem_class, elem_face, load_map, trace_map):
    subs, _, _, rhs, half = start.shape
    elems = elem_class.shape[1]
    classes = load_map.shape[0]
    count = start.size // rhs * lax.axis_size("slab") * lax.axis_size("sub")
    size = (ITERS + 1) * rhs
    full = 2 * half
    smem = pl.BlockSpec(memory_space=pltpu.SMEM)
    vmem = pl.BlockSpec(memory_space=pltpu.VMEM)
    hbm = pl.BlockSpec(memory_space=pltpu.HBM)

    def shape(*dims, dtype=F32):
        return jax.ShapeDtypeStruct(dims, dtype)

    sums = shape(start.shape[1] * subs, half, full)
    scratch = [pltpu.VMEM((GROUP, half, full), F32), pltpu.SMEM((subs * elems,), jnp.int32)]

    def call(kernel, out_shape, in_specs, scratch_shapes):
        return pl.pallas_call(
            kernel,
            out_shape=out_shape,
            in_specs=in_specs,
            out_specs=(vmem,) * len(out_shape),
            scratch_shapes=scratch_shapes,
            compiler_params=PARAMS,
            cost_estimate=pl.CostEstimate(
                flops=2 * 10**9, bytes_accessed=4 * 10**6, transcendentals=0
            ),
        )

    def shifted(x, axis, up):
        last = lax.axis_size(axis) - 1
        return lax.ppermute(x, axis, [(i, i + 1) if up else (i + 1, i) for i in range(last)])

    load = shape(subs, half + rhs + 16, full)
    far = [
        pltpu.with_memory_space_constraint(x, pltpu.HBM)
        for x in (elem_face, elem_class, partner, inv_factor, load_map, trace_map, start)
    ]
    to_sub, to_slab, held, first, last, sent_sum = call(
        compose_sent,
        (load, load, shape(*inv_factor.shape, dtype=BF16), shape(classes, half, full, dtype=BF16),
         shape(classes, full, full, dtype=BF16), sums),
        [hbm] * 7,
        scratch + [
            pltpu.VMEM(load_map.shape, BF16),
            pltpu.VMEM(trace_map.shape, BF16),
            pltpu.VMEM((subs, 2, rhs, half), F32),
            pltpu.VMEM((subs, 2, rhs, half), F32),
            pltpu.SMEM(elem_face.shape, jnp.int32),
            pltpu.SMEM(elem_class.shape, jnp.int32),
            pltpu.SMEM(partner.shape, jnp.int32),
            pltpu.SemaphoreType.DMA((7 + 4,)),
        ],
    )(*far)
    from_slab = shifted(to_slab, "slab", False)
    from_sub = shifted(to_sub, "sub", False)

    slots = 2 * subs
    square = shape(slots, full, full, dtype=BF16)
    rows = shape(slots, size, full, dtype=BF16)
    wide_high, wide_low, inner_high, inner_low, inner_gram = call(
        compose_kept,
        (square, square, rows, rows, shape(size, 128)),
        [smem, smem, smem, smem] + [vmem] * 5,
        [pltpu.VMEM(sums.shape, F32)] + scratch + [
            pltpu.VMEM((slots, full, full), BF16),
            pltpu.VMEM((slots, full, full), BF16),
            pltpu.VMEM((slots, rhs, full), F32),
            pltpu.VMEM((slots, rhs, full), F32),
        ],
    )(elem_face, elem_class, partner, partner_face, held, first, last, start, sent_sum)

    back = shape(subs, ITERS * rhs, full)
    gram, rows_high, rows_low, ret_sub, ret_slab = call(
        krylov,
        (shape(2 * rhs, 128), rows, rows, back, back),
        [smem] + [vmem] * 6,
        [
            pltpu.VMEM((slots, full, full), BF16),
            pltpu.VMEM((slots, full, full), BF16),
            pltpu.VMEM((slots, size, full), BF16),
            pltpu.VMEM((slots, size, full), BF16),
            pltpu.VMEM((2 * slots, rhs, full), F32),
            pltpu.VMEM((2 * slots, rhs, full), F32),
        ],
    )(partner, wide_high, wide_low, from_sub, from_slab, start, inner_gram)

    back_slab = shifted(ret_slab, "slab", True)
    back_sub = shifted(ret_sub, "sub", True)
    gram = summed(gram, ("sub", "slab"))

    return call(
        functools.partial(finish, float(count)),
        (shape(*start.shape), shape(ITERS, ITERS + 1, rhs, rhs)),
        [vmem] * 8,
        [
            pltpu.VMEM((128, 128), F32),
            pltpu.VMEM((128, 128), F32),
            pltpu.VMEM((slots, size, full), BF16),
            pltpu.VMEM((slots, size, full), BF16),
        ],
    )(gram, inner_high, inner_low, rows_high, rows_low, back_sub, back_slab, start)


def solution(mesh):
    placed = (
        P(("slab", "sub"), None, None, None, None),
        P(("slab", "sub"), None, None, None),
        P(("slab", "sub"), None),
        P(("slab", "sub"), None),
        P(("slab", "sub"), None),
        P(("slab", "sub"), None),
        P(),
        P(),
    )

    return jax.shard_map(
        body,
        mesh=mesh,
        in_specs=placed,
        out_specs=(P(("slab", "sub"), None, None, None, None), P()),
        check_vma=False,
    )
```

```python
import functools

import jax
import jax.numpy as jnp
from jax import lax
from jax.experimental import pallas as pl
from jax.experimental.pallas import tpu as pltpu
from jax.sharding import PartitionSpec as P


ITERS = 4
STEP_SCALE = 2.0**-8
INNER = (0, 1)
SHARED = (3, 5)
SENT = (2, 4)
GROUP = 8
LEAST = 2
ROWS = ((4, 1, 0), (3, 2))

F32 = jnp.float32
BF16 = jnp.bfloat16
HIGHEST = lax.Precision.HIGHEST
PARAMS = pltpu.CompilerParams(vmem_limit_bytes=24 * 2**20)


def dot(a, b, transposed=False, precision=None):
    dims = (((1,), (1 if transposed else 0,)), ((), ()))
    return lax.dot_general(a, b, dims, precision=precision, preferred_element_type=F32)


def two_parts(x):
    high = x.astype(BF16)
    return high, (x - high.astype(F32)).astype(BF16)


def embedded(real, imag):
    return jnp.concatenate(
        [jnp.concatenate([real, -imag], axis=1), jnp.concatenate([imag, real], axis=1)], axis=0
    )


def listed(face_ref, class_ref, order):
    subs, elems = face_ref.shape
    front, back = jnp.int32(0), jnp.int32(subs * elems - 1)
    for s in range(subs):
        for e in range(elems):
            face = face_ref[s, e]
            hit = (face == SENT[0]) | (face == SENT[1])
            order[jnp.where(hit, front, back)] = (
                (s * elems + e) * 4096 + (face * subs + s) * 64 + class_ref[s, e]
            )
            hit = hit.astype(jnp.int32)
            front, back = front + hit, back - 1 + hit
    return front


def groups(count):
    return (count + GROUP - 1) // GROUP


def stop_of(sent):
    return jnp.maximum(groups(sent), LEAST)


def compose(span, total, held, first_ref, last_ref, sum_ref, order, part):
    sum_ref[...] = jnp.zeros_like(sum_ref)

    def group(g, carry):
        words = [order[jnp.minimum(g * GROUP + u, total - 1)] for u in range(GROUP)]
        for u in range(GROUP):
            kind = words[u] & 63
            e = lax.shift_right_logical(words[u], 12)
            wide = embedded(held[e, 0], held[e, 1])
            out = dot(first_ref[kind], wide, True)
            out = dot(out.astype(BF16), wide)
            part[u] = dot(out.astype(BF16), last_ref[kind])
        for u in range(GROUP):
            at = lax.shift_right_logical(words[u], 6) & 63
            sum_ref[at] = sum_ref[at] + jnp.where(g * GROUP + u < total, part[u], 0.0)
        return carry

    lax.fori_loop(span[0], span[1], group, 0)


def pack(out_ref, operator_of, start_of, partner_ref, face, subs):
    for s in range(subs):
        real, imag = start_of(s)
        rhs, half = real.shape
        out_ref[s, :half] = operator_of(s)
        out_ref[s, half : half + rhs, :half] = real
        out_ref[s, half : half + rhs, half:] = imag
        partner = partner_ref[s, face]
        there = (partner >= 0).astype(F32)
        local = jnp.where(partner >= 0, partner % subs, 0).astype(F32)
        out_ref[s, half + rhs : half + rhs + 8] = jnp.full((8, 2 * half), local, F32)
        out_ref[s, half + rhs + 8 : half + rhs + 16] = jnp.full((8, 2 * half), there, F32)


def compose_sent(face_hbm, class_hbm, partner_hbm, inv_ref, load_ref, trace_ref, start_ref,
                 to_sub, to_slab, held, first_ref, last_ref, sum_ref, part, order,
                 load, trace, sub_rows, slab_rows, face_ref, class_ref, partner_ref, sems):
    subs = face_ref.shape[0]
    half = load_ref.shape[2]
    copies = []
    for source, place in (
        (load_ref, load),
        (trace_ref, trace),
        (face_hbm, face_ref),
        (class_hbm, class_ref),
        (start_ref.at[:, SENT[0]], sub_rows),
        (start_ref.at[:, SENT[1]], slab_rows),
        (partner_hbm, partner_ref),
    ):
        copies.append(pltpu.make_async_copy(source, place, sems.at[len(copies)]))
    small = len(copies)
    step = inv_ref.shape[0] // (sems.shape[0] - small)
    for i in range(sems.shape[0] - small):
        span = pl.ds(i * step, step)
        copies.append(
            pltpu.make_async_copy(inv_ref.at[span], held.at[span], sems.at[small + i])
        )
    for copy in copies:
        copy.start()
    for copy in copies[:2]:
        copy.wait()
    for c in range(load_ref.shape[0]):
        for x in range(2):
            first_ref[c, :, x * half : (x + 1) * half] = load[c, x].astype(F32).T.astype(BF16)
        real, imag = [trace[c, x].astype(F32).T.astype(BF16) for x in range(2)]
        last_ref[c] = embedded(real, -imag)
    for copy in copies[2:small]:
        copy.wait()
    stop = stop_of(listed(face_ref, class_ref, order))
    for copy in copies[small:]:
        copy.wait()
    compose((0, stop), held.shape[0], held, first_ref, last_ref, sum_ref, order, part)
    for out_ref, rows, face in ((to_sub, sub_rows, SENT[0]), (to_slab, slab_rows, SENT[1])):
        pack(out_ref, lambda s: sum_ref[face * subs + s], lambda s: (rows[s, 0], rows[s, 1]),
             partner_ref, face, subs)


def spread(rows):
    half = rows.shape[0]
    lower = jnp.concatenate([-rows[:, half:], rows[:, :half]], axis=1)
    return jnp.concatenate([rows, lower], axis=0).astype(BF16)


def leaving(high, low, x, wide):
    rhs = x.shape[0]
    both = dot(jnp.concatenate([high, low], axis=0), wide)
    return (both[:rhs] + both[rhs:] - x) * STEP_SCALE


def products(pairs):
    total = None
    for high, low in pairs:
        both = jnp.concatenate([high, low], axis=0)
        term = dot(both, both, True)
        total = term if total is None else total + term
    size = total.shape[0] // 2
    return (total[:size, :size] + total[size:, size:]) + (total[:size, size:] + total[size:, :size])


def compose_kept(face_ref, class_ref, partner_ref, partner_face_ref, held, first_ref, last_ref,
                 start_ref, sent_sum, wide_ref, rows_high, rows_low, gram_ref,
                 sum_ref, part, order, inner_wide, now_ref, out_ref):
    subs, _, _, rhs, _ = start_ref.shape
    faces = INNER + SHARED
    inner = len(INNER)
    stop = stop_of(listed(face_ref, class_ref, order))
    total = held.shape[0]
    compose((stop, groups(total)), total, held, first_ref, last_ref, sum_ref, order, part)
    for s in range(subs):
        for i, face in enumerate(faces):
            at = face * subs + s
            wide = spread(sent_sum[at] + sum_ref[at])
            if i < inner:
                inner_wide[s * inner + i] = wide
            else:
                wide_ref[(i - inner) * subs + s] = wide
    slots = subs * inner
    for s in range(subs):
        for f in INNER:
            value = jnp.concatenate([start_ref[s, f, 0], start_ref[s, f, 1]], axis=1)
            now_ref[s * inner + f] = value
            high, low = two_parts(value)
            rows_high[s * inner + f, :rhs] = high
            rows_low[s * inner + f, :rhs] = low
    for k in range(ITERS):
        now = slice(k * rhs, (k + 1) * rhs)
        later = slice((k + 1) * rhs, (k + 2) * rhs)
        for at in range(slots):
            out_ref[at] = leaving(rows_high[at, now], rows_low[at, now], now_ref[at],
                                  inner_wide[at])
        for s in range(subs):
            for f in INNER:
                local = partner_ref[s, f] % subs * inner + partner_face_ref[s, f]
                value = out_ref[0]
                for p in range(1, slots):
                    value = jnp.where(local == p, out_ref[p], value)
                now_ref[s * inner + f] = value
                high, low = two_parts(value)
                rows_high[s * inner + f, later] = high
                rows_low[s * inner + f, later] = low
    size = (ITERS + 1) * rhs
    gram_ref[:, :size] = products([(rows_high[at], rows_low[at]) for at in range(slots)])


def krylov(partner_ref, wide_ref, from_sub_ref, from_slab_ref, start_ref, inner_ref,
           gram_ref, rows_high, rows_low, to_sub_ref, to_slab_ref,
           far_wide, far_high, far_low, now_ref, out_ref):
    subs, _, _, rhs, half = start_ref.shape
    own = 2 * subs
    sources = (from_sub_ref, from_slab_ref)
    targets = (to_sub_ref, to_slab_ref)

    for d in range(2):
        for s in range(subs):
            at = d * subs + s
            face = SHARED[d]
            far_wide[at] = spread(sources[d][s, :half])
            value = jnp.concatenate([start_ref[s, face, 0], start_ref[s, face, 1]], axis=1)
            now_ref[at] = value
            rows_high[at, :rhs], rows_low[at, :rhs] = two_parts(value)
            value = sources[d][s, half : half + rhs]
            now_ref[own + at] = value
            far_high[at, :rhs], far_low[at, :rhs] = two_parts(value)

    for k in range(ITERS):
        now = slice(k * rhs, (k + 1) * rhs)
        later = slice((k + 1) * rhs, (k + 2) * rhs)
        for at in range(own):
            out_ref[at] = leaving(rows_high[at, now], rows_low[at, now], now_ref[at],
                                  wide_ref[at])
            out_ref[own + at] = leaving(far_high[at, now], far_low[at, now], now_ref[own + at],
                                        far_wide[at])
        for d in range(2):
            for s in range(subs):
                at = d * subs + s
                partner = partner_ref[s, SHARED[d]]
                local = partner % subs
                value = out_ref[own + d * subs]
                for p in range(1, subs):
                    value = jnp.where(local == p, out_ref[own + d * subs + p], value)
                value = jnp.where(partner >= 0, value, 0.0)
                now_ref[at] = value
                rows_high[at, later], rows_low[at, later] = two_parts(value)
                local = sources[d][s, half + rhs : half + rhs + 1]
                there = sources[d][s, half + rhs + 8 : half + rhs + 9]
                value = out_ref[d * subs]
                for p in range(1, subs):
                    value = jnp.where(local > p - 0.5, out_ref[d * subs + p], value)
                value = jnp.where(there > 0.5, value, 0.0)
                now_ref[own + at] = value
                far_high[at, later], far_low[at, later] = two_parts(value)
                targets[d][s, now] = value

    size = (ITERS + 1) * rhs
    total = inner_ref[:, :size] + products(
        [(rows_high[at], rows_low[at]) for at in range(own)]
        + [(far_high[at], far_low[at]) for at in range(own)]
    )
    alone = []
    for face in SENT:
        for s in range(subs):
            share = jnp.where(partner_ref[s, face] < 0, 1.0, 0.0)
            rows = jnp.concatenate([start_ref[s, face, 0], start_ref[s, face, 1]], axis=1)
            alone.append(two_parts(rows * share))
    first = total[:rhs, :rhs] + products(alone)

    gram_ref[...] = jnp.zeros_like(gram_ref)
    for row, blocks in enumerate(ROWS):
        lane = 0
        for i in blocks:
            width = (i + 1) * rhs
            piece = first if i == 0 else total[i * rhs : (i + 1) * rhs, :width]
            gram_ref[row * rhs : (row + 1) * rhs, lane : lane + width] = piece
            lane += width


def finish(count, gram_ref, inner_high, inner_low, rows_high, rows_low, back_sub_ref,
           back_slab_ref, start_ref, last_ref, hess_ref, upper_ref, inverse_ref, back_high, back_low):
    subs, _, _, rhs, half = start_ref.shape
    size = (ITERS + 1) * rhs
    lanes = 128
    for d, back_ref in enumerate((back_sub_ref, back_slab_ref)):
        for s in range(subs):
            at = d * subs + s
            first = jnp.concatenate([start_ref[s, SENT[d], 0], start_ref[s, SENT[d], 1]], axis=1)
            back_high[at, :rhs], back_low[at, :rhs] = two_parts(first)
            back_high[at, rhs:], back_low[at, rhs:] = two_parts(back_ref[s])

    upper_ref[...] = jnp.zeros_like(upper_ref)
    for row, blocks in enumerate(ROWS):
        lane = 0
        for i in blocks:
            width = (i + 1) * rhs
            upper_ref[i * rhs : (i + 1) * rhs, :width] = (
                gram_ref[row * rhs : (row + 1) * rhs, lane : lane + width] / count
            )
            lane += width
    lower = upper_ref[...]
    down = lax.broadcasted_iota(jnp.int32, (lanes, lanes), 0)
    across = lax.broadcasted_iota(jnp.int32, (lanes, lanes), 1)
    full = jnp.where(down >= across, lower, lower.T)

    blocks = size // 8
    work = [full[8 * i : 8 * i + 8] for i in range(blocks)]
    side = [
        (down[8 * i : 8 * i + 8] == across[8 * i : 8 * i + 8]).astype(F32) for i in range(blocks)
    ]
    sub_row = lax.broadcasted_iota(jnp.int32, (8, lanes), 0)

    def spread_row(x, r):
        return jnp.broadcast_to(x[r : r + 1], (8, lanes))

    for i in range(blocks):
        columns = {
            m: [jnp.broadcast_to(work[m][:, 8 * i + q : 8 * i + q + 1], (8, lanes)) for q in range(8)]
            for m in range(i, blocks)
        }
        own = list(columns[i])
        row, other = work[i], side[i]
        for r in range(8):
            pivot = spread_row(own[r], r)
            root = lax.rsqrt(pivot)
            scale = 1.0 / pivot
            chosen = sub_row == r
            factor = own[r]
            top, rest = spread_row(row, r), spread_row(other, r)
            j = 8 * i + r
            upper_ref[j : j + 1, :] = (top * root)[:1]
            inverse_ref[j : j + 1, :] = (rest * root)[:1]

            def cleared(x, x_row):
                x_row = x_row * scale
                return jnp.where(chosen, x_row, x - factor * x_row)

            row, other = cleared(row, top), cleared(other, rest)
            for q in range(r + 1, 8):
                own[q] = cleared(own[q], spread_row(own[q], r))
        tops = [spread_row(row, q) for q in range(8)]
        rests = [spread_row(other, q) for q in range(8)]
        for m in range(i + 1, blocks):
            terms = [columns[m][q] * tops[q] for q in range(8)]
            while len(terms) > 1:
                terms = [terms[q] + terms[q + 1] for q in range(0, len(terms), 2)]
            work[m] = work[m] - terms[0]
            terms = [columns[m][q] * rests[q] for q in range(8)]
            while len(terms) > 1:
                terms = [terms[q] + terms[q + 1] for q in range(0, len(terms), 2)]
            side[m] = side[m] - terms[0]
    upper_ref[size:, :] = jnp.zeros((lanes - size, lanes), F32)
    inverse_ref[size:, :] = jnp.zeros((lanes - size, lanes), F32)

    upper = jnp.where(down <= across, upper_ref[...], 0.0)
    inverse = jnp.where(down >= across, inverse_ref[...], 0.0)
    mix = inverse[ITERS * rhs : size, :size]
    mix_high, mix_low = two_parts(mix)
    mix_both = jnp.concatenate([mix_high, mix_low], axis=0)

    def put(s, face, high, low):
        value = dot(mix_both, high)
        value = value[:rhs] + value[rhs:] + dot(mix_high, low)
        last_ref[s, face, 0] = value[:, :half]
        last_ref[s, face, 1] = value[:, half:]

    for s in range(subs):
        for f in INNER:
            at = s * len(INNER) + f
            put(s, f, inner_high[at], inner_low[at])
        for d in range(2):
            at = d * subs + s
            put(s, SHARED[d], rows_high[at], rows_low[at])
            put(s, SENT[d], back_high[at], back_low[at])

    shifted = jnp.concatenate([upper[:, rhs:], jnp.zeros((lanes, rhs), F32)], axis=1)
    moved = dot(shifted, inverse, True, HIGHEST) * (1.0 / STEP_SCALE)
    unit = (down[:rhs, :rhs] == across[:rhs, :rhs]).astype(F32)
    for k in range(ITERS):
        for j in range(ITERS + 1):
            if j > k + 1:
                hess_ref[k, j] = jnp.zeros((rhs, rhs), F32)
                continue
            block = moved[j * rhs : (j + 1) * rhs, k * rhs : (k + 1) * rhs]
            block = block if (j + k) % 2 else -block
            hess_ref[k, j] = block + unit if j == k else block


def summed(x, axes):
    for axis in axes:
        count, stride = lax.axis_size(axis), 1
        while stride < count:
            rest = count // stride
            ways = next(p for p in range(2, rest + 1) if rest % p == 0)
            received = []
            for d in range(1, ways):
                pairs = []
                for i in range(count):
                    digit = (i // stride) % ways
                    pairs.append((i, i + ((digit + d) % ways - digit) * stride))
                received.append(lax.ppermute(x, axis, pairs))
            for y in received:
                x = x + y
            stride *= ways
    return x


def body(start, inv_factor, partner, partner_face, elem_class, elem_face, load_map, trace_map):
    subs, _, _, rhs, half = start.shape
    elems = elem_class.shape[1]
    classes = load_map.shape[0]
    count = start.size // rhs * lax.axis_size("slab") * lax.axis_size("sub")
    size = (ITERS + 1) * rhs
    full = 2 * half
    smem = pl.BlockSpec(memory_space=pltpu.SMEM)
    vmem = pl.BlockSpec(memory_space=pltpu.VMEM)
    hbm = pl.BlockSpec(memory_space=pltpu.HBM)

    def shape(*dims, dtype=F32):
        return jax.ShapeDtypeStruct(dims, dtype)

    sums = shape(start.shape[1] * subs, half, full)
    scratch = [pltpu.VMEM((GROUP, half, full), F32), pltpu.SMEM((subs * elems,), jnp.int32)]

    def call(kernel, out_shape, in_specs, scratch_shapes):
        return pl.pallas_call(
            kernel,
            out_shape=out_shape,
            in_specs=in_specs,
            out_specs=(vmem,) * len(out_shape),
            scratch_shapes=scratch_shapes,
            compiler_params=PARAMS,
            cost_estimate=pl.CostEstimate(
                flops=2 * 10**9, bytes_accessed=4 * 10**6, transcendentals=0
            ),
        )

    def shifted(x, axis, up):
        last = lax.axis_size(axis) - 1
        return lax.ppermute(x, axis, [(i, i + 1) if up else (i + 1, i) for i in range(last)])

    load = shape(subs, half + rhs + 16, full)
    far = [
        pltpu.with_memory_space_constraint(x, pltpu.HBM)
        for x in (elem_face, elem_class, partner, inv_factor, load_map, trace_map, start)
    ]
    to_sub, to_slab, held, first, last, sent_sum = call(
        compose_sent,
        (load, load, shape(*inv_factor.shape, dtype=BF16), shape(classes, half, full, dtype=BF16),
         shape(classes, full, full, dtype=BF16), sums),
        [hbm] * 7,
        scratch + [
            pltpu.VMEM(load_map.shape, BF16),
            pltpu.VMEM(trace_map.shape, BF16),
            pltpu.VMEM((subs, 2, rhs, half), F32),
            pltpu.VMEM((subs, 2, rhs, half), F32),
            pltpu.SMEM(elem_face.shape, jnp.int32),
            pltpu.SMEM(elem_class.shape, jnp.int32),
            pltpu.SMEM(partner.shape, jnp.int32),
            pltpu.SemaphoreType.DMA((7 + 4,)),
        ],
    )(*far)
    from_slab = shifted(to_slab, "slab", False)
    from_sub = shifted(to_sub, "sub", False)

    slots = 2 * subs
    square = shape(slots, full, full, dtype=BF16)
    rows = shape(slots, size, full, dtype=BF16)
    wide, inner_high, inner_low, inner_gram = call(
        compose_kept,
        (square, rows, rows, shape(size, 128)),
        [smem, smem, smem, smem] + [vmem] * 5,
        [pltpu.VMEM(sums.shape, F32)] + scratch + [
            pltpu.VMEM((slots, full, full), BF16),
            pltpu.VMEM((slots, rhs, full), F32),
            pltpu.VMEM((slots, rhs, full), F32),
        ],
    )(elem_face, elem_class, partner, partner_face, held, first, last, start, sent_sum)

    back = shape(subs, ITERS * rhs, full)
    gram, rows_high, rows_low, ret_sub, ret_slab = call(
        krylov,
        (shape(2 * rhs, 128), rows, rows, back, back),
        [smem] + [vmem] * 5,
        [
            pltpu.VMEM((slots, full, full), BF16),
            pltpu.VMEM((slots, size, full), BF16),
            pltpu.VMEM((slots, size, full), BF16),
            pltpu.VMEM((2 * slots, rhs, full), F32),
            pltpu.VMEM((2 * slots, rhs, full), F32),
        ],
    )(partner, wide, from_sub, from_slab, start, inner_gram)

    back_slab = shifted(ret_slab, "slab", True)
    back_sub = shifted(ret_sub, "sub", True)
    gram = summed(gram, ("sub", "slab"))

    return call(
        functools.partial(finish, float(count)),
        (shape(*start.shape), shape(ITERS, ITERS + 1, rhs, rhs)),
        [vmem] * 8,
        [
            pltpu.VMEM((128, 128), F32),
            pltpu.VMEM((128, 128), F32),
            pltpu.VMEM((slots, size, full), BF16),
            pltpu.VMEM((slots, size, full), BF16),
        ],
    )(gram, inner_high, inner_low, rows_high, rows_low, back_sub, back_slab, start)


def solution(mesh):
    placed = (
        P(("slab", "sub"), None, None, None, None),
        P(("slab", "sub"), None, None, None),
        P(("slab", "sub"), None),
        P(("slab", "sub"), None),
        P(("slab", "sub"), None),
        P(("slab", "sub"), None),
        P(),
        P(),
    )

    return jax.shard_map(
        body,
        mesh=mesh,
        in_specs=placed,
        out_specs=(P(("slab", "sub"), None, None, None, None), P()),
        check_vma=False,
    )
```
